32 devices in a mesh: pipe: 4 (over x, core), tensor: 8 (over z, y).
Axes of the slice: x: 2, y: 2, z: 4, core: 2. Of those that a mesh axis runs over, the one named last changes fastest.
Arguments:
- hidden: bfloat16 [384, 8192], P('pipe', 'tensor'), may hold values from -64 to 64
- weight: bfloat16 [8192, 16384], P(None, ('pipe', 'tensor')), may hold values from -0.23201941 to 0.23201941
- targets: int32 [384], replicated, may hold values from 0 to 16383
- token_weight: float32 [384], replicated, may hold values from 0.1 to 1
Outputs:
- token_loss: float32 [384], P('pipe')
- hidden_grad: float32 [384, 8192], P('pipe', 'tensor')
The draws below stay inside these ranges and needn't reach their ends.
All inputs are finite; a program needn't handle non-finite values.
Results may differ from the reference program's by a relative error of at most 0.0029.
Values may be sent and summed in bfloat16 or wider, within the bound.
A program may use at most 128 MiB of HBM per device.

```python
import math
import jax
import jax.numpy as jnp

D = 8192
TOKENS = 384
VOCAB = 16384


scale_base = 3.0


def weight_table(key):
    key_entries = jax.random.fold_in(key, 11)
    key_columns = jax.random.fold_in(key, 12)
    entries = jnp.clip(jax.random.normal(key_entries, (D, VOCAB), jnp.float32), -5.0, 5.0)
    ramp = 0.87 + 0.26 * jnp.arange(VOCAB, dtype=jnp.float32) / VOCAB
    jitter = jax.random.uniform(key_columns, (VOCAB,), jnp.float32, 0.8, 1.2)
    column_scale = ramp * jitter * scale_base / math.sqrt(D)
    return (entries * column_scale[None, :]).astype(jnp.bfloat16)


def draw_weight(key, part):
    return weight_table(key)


def draw_hidden(key, part):
    key_rows = jax.random.fold_in(key, 21)
    base = jnp.clip(jax.random.normal(key_rows, (TOKENS, D), jnp.float32), -6.0, 6.0)
    return base.astype(jnp.bfloat16)


def set_ends(values, key, low, high):
    longest = values.shape.index(max(values.shape))
    spots = []
    for shift in (0, 1):
        where = [jax.random.randint(jax.random.fold_in(key, axis), (), 0, length) for axis, length in enumerate(values.shape)]
        where[longest] = (where[longest] + shift) % values.shape[longest]
        spots.append(tuple(where))
    return values.at[spots[0]].set(low).at[spots[1]].set(high)


def setup_inputs(seed: int = 0) -> dict:
    splits = jax.random.split(jax.random.key(seed), 5)
    hidden = draw_hidden(jax.random.fold_in(splits[4], 71), 0)
    weight = draw_weight(jax.random.fold_in(splits[4], 71), 0)
    targets = set_ends(jax.random.randint(splits[2], (TOKENS,), 0, VOCAB), jax.random.fold_in(splits[2], 1), 0, VOCAB - 1).astype(jnp.int32)
    token_weight = jnp.clip(jnp.exp(jax.random.uniform(splits[3], (TOKENS,), jnp.float32, math.log(0.1), math.log(1.0))), 0.1, 1.0)
    return dict(hidden=hidden, weight=weight, targets=targets, token_weight=token_weight)


loss_scale = 32.0


def reference(hidden, weight, targets, token_weight):
    logits = jnp.dot(hidden, weight, preferred_element_type=jnp.float32)
    global_peak = jnp.max(logits, axis=1)
    global_total = jnp.sum(jnp.exp(logits - global_peak[:, None]), axis=1)
    log_total = global_peak + jnp.log(global_total)
    columns = jnp.arange(VOCAB, dtype=jnp.int32)
    target_hit = targets[:, None] == columns[None, :]
    target_logit = jnp.sum(jnp.where(target_hit, logits, jnp.float32(0.0)), axis=1)
    token_loss = log_total - target_logit
    softmax = jnp.exp(logits - log_total[:, None])
    onehot = target_hit.astype(jnp.float32)
    dlogits = (loss_scale * token_weight[:, None] * (softmax - onehot)).astype(jnp.bfloat16)
    hidden_grad = jnp.dot(dlogits, weight.T, preferred_element_type=jnp.float32)
    return token_loss, hidden_grad
```

```python
import functools

import jax
import jax.numpy as jnp
from jax import lax
from jax.experimental import pallas as pl
from jax.experimental.pallas import tpu as pltpu
from jax.sharding import PartitionSpec as P

loss_scale = 32.0
f32, bf16 = jnp.float32, jnp.bfloat16
MESH = pl.DeviceIdType.MESH


def flat_rows(block):
    n, rows, width = block.shape
    if rows % 16:
        return block.astype(f32).reshape(n * rows, width).astype(bf16)
    return block.reshape(n * rows, width)


def to_column(row):
    return jnp.transpose(jnp.broadcast_to(row, (128, row.shape[1])))[:, :1]


def merge(parts):
    peak = functools.reduce(jnp.maximum, [part[0:1] for part in parts])
    total = sum(part[1:2] * jnp.exp(part[0:1] - peak) for part in parts)
    chosen = sum(part[2:3] for part in parts)
    return jnp.concatenate([peak, total, chosen, jnp.zeros_like(peak)], axis=0)


def kernel(
    nA, nB, nC,
    hidden, weight, targets, token_weight,
    loss_out, grad_out,
    H, W, acc, dl, Pb, Sib, x1b, x1r, y1b, y1r, x2b, x2r, y2b, y2r, zb, zr, keep, stb, st,
    wsem, hsem, gz, gx1, gy1, gx2, gy2, gs, rs, rx1, ry1, rx2, ry2, rz, ssem,
):
    rows, cols = hidden.shape
    half = cols // 2
    lo, hi = pl.ds(0, half), pl.ds(half, half)
    p, t = lax.axis_index("pipe"), lax.axis_index("tensor")
    a, c = p // 2, lax.rem(p, 2)
    b, z = lax.rem(t, nB), t // nB

    def at(a_=None, b_=None, z_=None, c_=None):
        a_, b_ = (a if a_ is None else a_), (b if b_ is None else b_)
        z_, c_ = (z if z_ is None else z_), (c if c_ is None else c_)
        return {"pipe": a_ * 2 + c_, "tensor": z_ * nB + b_}

    As = [lax.rem(a + o, nA) for o in range(1, nA)]
    Bs = [lax.rem(b + o, nB) for o in range(1, nB)]
    Zs = [lax.rem(z - o + nC, nC) for o in range(1, nC)]
    sib = at(c_=1 - c)
    peers = [sib] + [at(a_=i) for i in As] + [at(b_=i) for i in Bs] + [at(z_=i) for i in Zs]

    def put(src, dst, sems, here, there, dev):
        pltpu.make_async_remote_copy(
            src_ref=src, dst_ref=dst, send_sem=sems[0].at[here], recv_sem=sems[1].at[there],
            device_id=dev, device_id_type=MESH,
        ).start()

    def got(dst, sems, there):
        pltpu.make_async_remote_copy(
            src_ref=dst, dst_ref=dst, send_sem=sems[0].at[there], recv_sem=sems[1].at[there],
            device_id=sib, device_id_type=MESH,
        ).wait_recv()

    def sent(src, sems, here):
        pltpu.make_async_remote_copy(
            src_ref=src, dst_ref=src, send_sem=sems[0].at[here], recv_sem=sems[1].at[here],
            device_id=sib, device_id_type=MESH,
        ).wait_send()

    wcopy = pltpu.make_async_copy(weight, W, wsem)
    wcopy.start()
    hcopy = pltpu.make_async_copy(hidden, H.at[t, p], hsem)
    hcopy.start()
    barrier = pltpu.get_barrier_semaphore()
    for dev in peers:
        pl.semaphore_signal(barrier, inc=1, device_id=dev, device_id_type=MESH)
    pl.semaphore_wait(barrier, len(peers))

    def slot(k, b_, a_, c_=None):
        return H.at[k * nB + b_, a_ * 2 + (c if c_ is None else c_)]

    for k in Zs:
        put(hidden, slot(z, b, a), gz, k, z, at(z_=k))
    hcopy.wait()
    acc[...] = jnp.zeros_like(acc)

    def spread(i):
        k = lax.rem(z + i, nC)

        @pl.when(i > 0)
        def _():
            got(slot(k, b, a), gz, k)

        own = slot(k, b, a)
        for j in As:
            put(own, own, gx1, (k, j), (k, a), at(a_=j))
        for j in Bs:
            put(own, own, gy1, (k, j), (k, b), at(b_=j))
        put(own, own, gs, (k, b, a), (k, b, a), sib)

    def forward(i):
        k = lax.rem(z + i, nC)
        for j in As:
            blk = slot(k, b, j)
            got(blk, gx1, (k, j))
            for m in Bs:
                put(blk.at[:, lo], blk.at[:, lo], gy2, (k, m, j), (k, b, j), at(b_=m))
        for j in Bs:
            blk = slot(k, j, a)
            got(blk, gy1, (k, j))
            for m in As:
                put(blk.at[:, hi], blk.at[:, hi], gx2, (k, j, m), (k, j, a), at(a_=m))
        for j in As:
            blk = slot(k, b, j)
            put(blk, blk, gs, (k, b, j), (k, b, j), sib)
        for j in Bs:
            blk = slot(k, j, a)
            put(blk, blk, gs, (k, j, a), (k, j, a), sib)

    def finish(i):
        k = lax.rem(z + i, nC)
        for j in As:
            for m in Bs:
                blk = slot(k, m, j)
                got(blk.at[:, lo], gy2, (k, m, j))
                got(blk.at[:, hi], gx2, (k, m, j))
                put(blk, blk, gs, (k, m, j), (k, m, j), sib)

    def multiply(i):
        k = lax.rem(z + i, nC)
        for b_ in range(nB):
            for a_ in range(nA):
                got(slot(k, b_, a_, 1 - c), gs, (k, b_, a_))
        for b_ in range(nB):
            tt = k * nB + b_
            acc[...] += jnp.dot(flat_rows(H[tt]), W[tt], preferred_element_type=f32)

    spread(0)

    def gather_step(i, carry):
        @pl.when(i < nC)
        def _():
            forward(i)

        @pl.when(i < nC - 1)
        def _():
            spread(i + 1)

        @pl.when(i == 1)
        def _():
            wcopy.wait()

        @pl.when(i > 0)
        def _():
            finish(i - 1)
            multiply(i - 1)

        return carry

    lax.fori_loop(0, nC + 1, gather_step, 0)

    logits = acc[...]
    tokens, width = logits.shape
    device_block = p * lax.axis_size("tensor") + t
    target_col = to_column(targets[...].astype(f32)).astype(jnp.int32)
    columns = device_block * width + lax.broadcasted_iota(jnp.int32, (tokens, width), 1)
    hit = target_col == columns
    peak = jnp.max(logits, axis=1, keepdims=True)
    total = jnp.sum(jnp.exp(logits - peak), axis=1, keepdims=True)
    chosen = jnp.sum(jnp.where(hit, logits, 0.0), axis=1, keepdims=True)
    lane = lax.broadcasted_iota(jnp.int32, (tokens, 128), 1)
    packed = jnp.where(lane == 0, peak, jnp.where(lane == 1, total, jnp.where(lane == 2, chosen, 0.0)))
    cur = jnp.transpose(packed)[0:4]
    offset = 0
    for group, me, name in (([1 - c], c, "c_"), (Bs, b, "b_"), (As, a, "a_"), (Zs, z, "z_")):
        size = len(group) + 1
        stage = {"c_": 0, "b_": 1, "a_": 2, "z_": 3}[name]
        stb[stage] = cur
        for j in group:
            put(stb.at[stage], st.at[offset + me], ssem, offset + j, offset + me, at(**{name: j}))
        for j in group:
            got(st.at[offset + j], ssem, offset + j)
        cur = merge([cur] + [st[offset + j] for j in group])
        for j in group:
            sent(stb.at[stage], ssem, offset + j)
        offset += size
    log_total = cur[0:1] + jnp.log(cur[1:2])
    loss_out[...] = log_total - cur[2:3]
    softmax = jnp.exp(acc[...] - to_column(log_total))
    scale = loss_scale * to_column(token_weight[...])
    dl[...] = (scale * (softmax - hit.astype(f32))).astype(bf16)

    def order(i):
        return lax.rem(z + 1 + i, nC)

    def produce(i):
        k = order(i)
        for b_ in range(nB):
            tt = k * nB + b_
            for part in (lo, hi):
                term = lax.dot_general(
                    dl[...], W[tt, part, :], (((1,), (1,)), ((), ())), preferred_element_type=f32
                )
                Pb[tt, :, :, :, part] = term.reshape(nA, 2, rows, half)
            put(Pb.at[tt, :, 1 - c], Sib.at[tt], rs, tt, tt, sib)

    def stage1(i):
        k = order(i)
        for b_ in range(nB):
            tt = k * nB + b_
            got(Sib.at[tt], rs, tt)
            for a_ in range(nA):
                Sib[tt, a_] = Sib[tt, a_] + Pb[tt, a_, c]
        for j in As:
            for b_ in range(nB):
                x1b[k, j, b_] = Sib[k * nB + b_, j, :, lo].astype(bf16)
            put(x1b.at[k, j], x1r.at[k, a], rx1, (k, j), (k, a), at(a_=j))
        for j in Bs:
            for a_ in range(nA):
                y1b[k, j, a_] = Sib[k * nB + j, a_, :, hi].astype(bf16)
            put(y1b.at[k, j], y1r.at[k, b], ry1, (k, j), (k, b), at(b_=j))

    def stage2(i):
        k = order(i)
        for j in As:
            got(x1r.at[k, j], rx1, (k, j))
        for j in Bs:
            y2b[k, j] = (Sib[k * nB + j, a, :, lo] + sum(x1r[k, m, j].astype(f32) for m in As)).astype(bf16)
            put(y2b.at[k, j], y2r.at[k, b], ry2, (k, j), (k, b), at(b_=j))
        keep[:, lo] = Sib[k * nB + b, a, :, lo] + sum(x1r[k, m, b].astype(f32) for m in As)
        for j in Bs:
            got(y1r.at[k, j], ry1, (k, j))
        for j in As:
            x2b[k, j] = (Sib[k * nB + b, j, :, hi] + sum(y1r[k, m, j].astype(f32) for m in Bs)).astype(bf16)
            put(x2b.at[k, j], x2r.at[k, a], rx2, (k, j), (k, a), at(a_=j))
        keep[:, hi] = Sib[k * nB + b, a, :, hi] + sum(y1r[k, m, a].astype(f32) for m in Bs)
        Sib[k * nB + b, a] = keep[...]

    def stage3(i):
        k = order(i)
        for j in Bs:
            got(y2r.at[k, j], ry2, (k, j))
        for j in As:
            got(x2r.at[k, j], rx2, (k, j))
        keep[:, lo] = Sib[k * nB + b, a, :, lo] + sum(y2r[k, j].astype(f32) for j in Bs)
        keep[:, hi] = Sib[k * nB + b, a, :, hi] + sum(x2r[k, j].astype(f32) for j in As)

        @pl.when(i < nC - 1)
        def _():
            zb[k] = keep[...].astype(bf16)
            put(zb.at[k], zr.at[z], rz, k, z, at(z_=k))

    def reduce_step(i, carry):
        @pl.when(i < nC)
        def _():
            produce(i)

        @pl.when((i > 0) & (i < nC + 1))
        def _():
            stage1(i - 1)

        @pl.when((i > 1) & (i < nC + 2))
        def _():
            stage2(i - 2)

        @pl.when(i > 2)
        def _():
            stage3(i - 3)

        return carry

    lax.fori_loop(0, nC + 3, reduce_step, 0)
    for k in Zs:
        got(zr.at[k], rz, k)
    grad_out[...] = keep[...] + sum(zr[k].astype(f32) for k in Zs)

    for k in Zs:
        sent(hidden, gz, k)
        sent(zb.at[k], rz, k)

    def drain(k, carry):
        own = slot(k, b, a)
        for j in As:
            sent(own, gx1, (k, j))
            sent(x1b.at[k, j], rx1, (k, j))
            sent(x2b.at[k, j], rx2, (k, j))
        for j in Bs:
            sent(own, gy1, (k, j))
            sent(y1b.at[k, j], ry1, (k, j))
            sent(y2b.at[k, j], ry2, (k, j))
            for m in As:
                sent(own.at[:, lo], gy2, (k, j, m))
                sent(own.at[:, hi], gx2, (k, j, m))
        for b_ in range(nB):
            for a_ in range(nA):
                sent(own, gs, (k, b_, a_))
            sent(Sib.at[k * nB + b_], rs, k * nB + b_)
        return carry

    lax.fori_loop(0, nC, drain, 0)


def local(hidden, weight, targets, token_weight):
    rows, cols = hidden.shape
    n_pipe, n_tensor = lax.axis_size("pipe"), lax.axis_size("tensor")
    nA, nB, nC = n_pipe // 2, 2, n_tensor // 2
    tokens, width = targets.shape[0], weight.shape[1]
    half = cols // 2
    vmem, dma = pltpu.VMEM, pltpu.SemaphoreType.DMA
    sems = lambda *shape: [dma(shape), dma(shape)]
    groups = 2 + nA + nB + nC
    loss_rows, hidden_grad = pl.pallas_call(
        functools.partial(kernel, nA, nB, nC),
        out_shape=(
            jax.ShapeDtypeStruct((1, tokens), f32),
            jax.ShapeDtypeStruct((rows, cols), f32),
        ),
        in_specs=[
            pl.BlockSpec(memory_space=pl.ANY),
            pl.BlockSpec(memory_space=pl.ANY),
            pl.BlockSpec(memory_space=vmem),
            pl.BlockSpec(memory_space=vmem),
        ],
        out_specs=[pl.BlockSpec(memory_space=vmem)] * 2,
        scratch_shapes=[
            vmem((n_tensor, n_pipe, rows, cols), bf16),
            vmem((n_tensor, cols, width), bf16),
            vmem((tokens, width), f32),
            vmem((tokens, width), bf16),
            vmem((n_tensor, nA, 2, rows, cols), f32),
            vmem((n_tensor, nA, rows, cols), f32),
            vmem((nC, nA, nB, rows, half), bf16),
            vmem((nC, nA, nB, rows, half), bf16),
            vmem((nC, nB, nA, rows, half), bf16),
            vmem((nC, nB, nA, rows, half), bf16),
            vmem((nC, nA, rows, half), bf16),
            vmem((nC, nA, rows, half), bf16),
            vmem((nC, nB, rows, half), bf16),
            vmem((nC, nB, rows, half), bf16),
            vmem((nC, rows, cols), bf16),
            vmem((nC, rows, cols), bf16),
            vmem((rows, cols), f32),
            vmem((4, 4, tokens), f32),
            vmem((groups, 4, tokens), f32),
            dma,
            dma,
            sems(nC),
            sems(nC, nA),
            sems(nC, nB),
            sems(nC, nB, nA),
            sems(nC, nB, nA),
            sems(nC, nB, nA),
            sems(n_tensor),
            sems(nC, nA),
            sems(nC, nB),
            sems(nC, nA),
            sems(nC, nB),
            sems(nC),
            sems(groups),
        ],
        compiler_params=pltpu.CompilerParams(
            collective_id=0, has_side_effects=True, vmem_limit_bytes=62 * 1024 * 1024
        ),
    )(
        hidden,
        weight.reshape(n_tensor, cols, width),
        targets.reshape(1, tokens),
        token_weight.reshape(1, tokens),
    )
    token_loss = lax.dynamic_slice_in_dim(loss_rows[0], lax.axis_index("pipe") * rows, rows, 0)
    return token_loss, hidden_grad


def solution(mesh):
    in_specs = (P("pipe", "tensor"), P(None, ("pipe", "tensor")), P(), P())
    out_specs = (P("pipe"), P("pipe", "tensor"))
    return jax.shard_map(local, mesh=mesh, in_specs=in_specs, out_specs=out_specs, check_vma=False)
```

```python
import functools

import jax
import jax.numpy as jnp
from jax import lax
from jax.experimental import pallas as pl
from jax.experimental.pallas import tpu as pltpu
from jax.sharding import PartitionSpec as P

loss_scale = 32.0
f32, bf16 = jnp.float32, jnp.bfloat16
MESH = pl.DeviceIdType.MESH


def flat_rows(block):
    n, rows, width = block.shape
    if rows % 16:
        return block.astype(f32).reshape(n * rows, width).astype(bf16)
    return block.reshape(n * rows, width)


def to_column(row):
    return jnp.transpose(jnp.broadcast_to(row, (128, row.shape[1])))[:, :1]


def merge(parts):
    peak = functools.reduce(jnp.maximum, [part[0:1] for part in parts])
    total = sum(part[1:2] * jnp.exp(part[0:1] - peak) for part in parts)
    chosen = sum(part[2:3] for part in parts)
    return jnp.concatenate([peak, total, chosen, jnp.zeros_like(peak)], axis=0)


def kernel(
    nA, nB, nC,
    hidden, weight, targets, token_weight,
    loss_out, grad_out,
    H, W, acc, dl, Pb, Sib, x1b, x1r, y1b, y1r, x2b, x2r, y2b, y2r, zb, zr, keep, stb, st,
    wsem, hsem, gz, gx1, gy1, gx2, gy2, gs, rs, rx1, ry1, rx2, ry2, rz, ssem,
):
    rows, cols = hidden.shape
    half = cols // 2
    lo, hi = pl.ds(0, half), pl.ds(half, half)
    p, t = lax.axis_index("pipe"), lax.axis_index("tensor")
    a, c = p // 2, lax.rem(p, 2)
    b, z = lax.rem(t, nB), t // nB

    def at(a_=None, b_=None, z_=None, c_=None):
        a_, b_ = (a if a_ is None else a_), (b if b_ is None else b_)
        z_, c_ = (z if z_ is None else z_), (c if c_ is None else c_)
        return {"pipe": a_ * 2 + c_, "tensor": z_ * nB + b_}

    As = [lax.rem(a + o, nA) for o in range(1, nA)]
    Bs = [lax.rem(b + o, nB) for o in range(1, nB)]
    Zs = [lax.rem(z - o + nC, nC) for o in range(1, nC)]
    sib = at(c_=1 - c)
    Plane = [
        ((a_ * nB + b_) * 2 + c_, at(a_=a_, b_=b_, c_=c_))
        for a_ in [a] + As for b_ in [b] + Bs for c_ in (c, 1 - c)
    ][1:]
    peers = [dev for _, dev in Plane] + [at(z_=i) for i in Zs]

    def put(src, dst, sems, here, there, dev):
        pltpu.make_async_remote_copy(
            src_ref=src, dst_ref=dst, send_sem=sems[0].at[here], recv_sem=sems[1].at[there],
            device_id=dev, device_id_type=MESH,
        ).start()

    def got(dst, sems, there):
        pltpu.make_async_remote_copy(
            src_ref=dst, dst_ref=dst, send_sem=sems[0].at[there], recv_sem=sems[1].at[there],
            device_id=sib, device_id_type=MESH,
        ).wait_recv()

    def sent(src, sems, here):
        pltpu.make_async_remote_copy(
            src_ref=src, dst_ref=src, send_sem=sems[0].at[here], recv_sem=sems[1].at[here],
            device_id=sib, device_id_type=MESH,
        ).wait_send()

    wcopy = pltpu.make_async_copy(weight, W, wsem)
    wcopy.start()
    hcopy = pltpu.make_async_copy(hidden, H.at[t, p], hsem)
    hcopy.start()
    barrier = pltpu.get_barrier_semaphore()
    for dev in peers:
        pl.semaphore_signal(barrier, inc=1, device_id=dev, device_id_type=MESH)
    pl.semaphore_wait(barrier, len(peers))

    def slot(k, b_, a_, c_=None):
        return H.at[k * nB + b_, a_ * 2 + (c if c_ is None else c_)]

    hcopy.wait()
    acc[...] = jnp.zeros_like(acc)
    left, right = z, nC - 1 - z
    both = jnp.minimum(left, right)
    longer = jnp.where(left > right, -1, 1)

    def nearest(i):
        d = (i + 1) // 2
        turn = jnp.where(lax.rem(i, 2) == 1, -d, d)
        return z + jnp.where(i <= 2 * both, turn, longer * (i - both))

    def spread(i):
        k = nearest(i)
        own = slot(k, b, a)

        @pl.when(k != z)
        def _():
            got(own, gz, (k, 0))

        @pl.when((k <= z) & (z < nC - 1))
        def _():
            put(own, own, gz, (k, 1), (k, 0), at(z_=z + 1))

        @pl.when((k >= z) & (z > 0))
        def _():
            put(own, own, gz, (k, 0), (k, 0), at(z_=z - 1))

        for j in As:
            put(own, own, gx1, (k, j), (k, a), at(a_=j))
        for j in Bs:
            put(own, own, gy1, (k, j), (k, b), at(b_=j))
        put(own, own, gs, (k, b, a), (k, b, a), sib)

    def forward(i):
        k = nearest(i)
        for j in As:
            blk = slot(k, b, j)
            got(blk, gx1, (k, j))
            for m in Bs:
                put(blk.at[:, lo], blk.at[:, lo], gy2, (k, m, j), (k, b, j), at(b_=m))
        for j in Bs:
            blk = slot(k, j, a)
            got(blk, gy1, (k, j))
            for m in As:
                put(blk.at[:, hi], blk.at[:, hi], gx2, (k, j, m), (k, j, a), at(a_=m))
        for j in As:
            blk = slot(k, b, j)
            put(blk, blk, gs, (k, b, j), (k, b, j), sib)
        for j in Bs:
            blk = slot(k, j, a)
            put(blk, blk, gs, (k, j, a), (k, j, a), sib)

    def finish(i):
        k = nearest(i)
        for j in As:
            for m in Bs:
                blk = slot(k, m, j)
                got(blk.at[:, lo], gy2, (k, m, j))
                got(blk.at[:, hi], gx2, (k, m, j))
                put(blk, blk, gs, (k, m, j), (k, m, j), sib)

    def multiply(i):
        k = nearest(i)
        for b_ in range(nB):
            for a_ in range(nA):
                got(slot(k, b_, a_, 1 - c), gs, (k, b_, a_))
        for b_ in range(nB):
            tt = k * nB + b_
            acc[...] += jnp.dot(flat_rows(H[tt]), W[tt], preferred_element_type=f32)

    spread(0)

    def gather_step(i, carry):
        @pl.when(i < nC - 1)
        def _():
            spread(i + 1)

        @pl.when(i < nC)
        def _():
            forward(i)

        @pl.when(i == 2)
        def _():
            wcopy.wait()

        @pl.when(i > 1)
        def _():
            finish(i - 2)
            multiply(i - 2)

        return carry

    lax.fori_loop(0, nC + 2, gather_step, 0)

    logits = acc[...]
    tokens, width = logits.shape
    device_block = p * lax.axis_size("tensor") + t
    target_col = to_column(targets[...].reshape(1, tokens).astype(f32)).astype(jnp.int32)
    columns = device_block * width + lax.broadcasted_iota(jnp.int32, (tokens, width), 1)
    hit = target_col == columns
    peak = jnp.max(logits, axis=1, keepdims=True)
    total = jnp.sum(jnp.exp(logits - peak), axis=1, keepdims=True)
    chosen = jnp.sum(jnp.where(hit, logits, 0.0), axis=1, keepdims=True)
    lane = lax.broadcasted_iota(jnp.int32, (tokens, 128), 1)
    packed = jnp.where(lane == 0, peak, jnp.where(lane == 1, total, jnp.where(lane == 2, chosen, 0.0)))
    cur = jnp.transpose(packed)[0:4]
    plane = nA * nB * 2
    here = (a * nB + b) * 2 + c
    for stage, group, base, me in ((0, Plane, 0, here), (1, [(k, at(z_=k)) for k in Zs], plane, z)):
        stb[stage] = cur
        for j, dev in group:
            put(stb.at[stage], st.at[base + me], ssem, base + j, base + me, dev)
        for j, _ in group:
            got(st.at[base + j], ssem, base + j)
        cur = merge([cur] + [st[base + j] for j, _ in group])
        for j, _ in group:
            sent(stb.at[stage], ssem, base + j)
    log_total = cur[0:1] + jnp.log(cur[1:2])
    loss = jnp.broadcast_to(log_total - cur[2:3], (8, tokens))
    loss_out[...] = pltpu.roll(loss, lax.rem(tokens - p * rows, tokens), axis=1)[0, :rows]
    softmax = jnp.exp(acc[...] - to_column(log_total))
    scale = loss_scale * to_column(token_weight[...].reshape(1, tokens))
    dl[...] = (scale * (softmax - hit.astype(f32))).astype(bf16)

    def order(i):
        return lax.rem(z + 1 + i, nC)

    def produce(i):
        k = order(i)
        for b_ in range(nB):
            tt = k * nB + b_
            for part in (lo, hi):
                term = lax.dot_general(
                    dl[...], W[tt, part, :], (((1,), (1,)), ((), ())), preferred_element_type=f32
                )
                Pb[tt, :, :, :, part] = term.reshape(nA, 2, rows, half)
            put(Pb.at[tt, :, 1 - c], Sib.at[tt], rs, tt, tt, sib)

    def stage1(i):
        k = order(i)
        for b_ in range(nB):
            tt = k * nB + b_
            got(Sib.at[tt], rs, tt)
            for a_ in range(nA):
                Sib[tt, a_] = Sib[tt, a_] + Pb[tt, a_, c]
        for j in As:
            for b_ in range(nB):
                x1b[k, j, b_] = Sib[k * nB + b_, j, :, lo].astype(bf16)
            put(x1b.at[k, j], x1r.at[k, a], rx1, (k, j), (k, a), at(a_=j))
        for j in Bs:
            for a_ in range(nA):
                y1b[k, j, a_] = Sib[k * nB + j, a_, :, hi].astype(bf16)
            put(y1b.at[k, j], y1r.at[k, b], ry1, (k, j), (k, b), at(b_=j))

    def stage2(i):
        k = order(i)
        for j in As:
            got(x1r.at[k, j], rx1, (k, j))
        for j in Bs:
            y2b[k, j] = (Sib[k * nB + j, a, :, lo] + sum(x1r[k, m, j].astype(f32) for m in As)).astype(bf16)
            put(y2b.at[k, j], y2r.at[k, b], ry2, (k, j), (k, b), at(b_=j))
        keep[:, lo] = Sib[k * nB + b, a, :, lo] + sum(x1r[k, m, b].astype(f32) for m in As)
        for j in Bs:
            got(y1r.at[k, j], ry1, (k, j))
        for j in As:
            x2b[k, j] = (Sib[k * nB + b, j, :, hi] + sum(y1r[k, m, j].astype(f32) for m in Bs)).astype(bf16)
            put(x2b.at[k, j], x2r.at[k, a], rx2, (k, j), (k, a), at(a_=j))
        keep[:, hi] = Sib[k * nB + b, a, :, hi] + sum(y1r[k, m, a].astype(f32) for m in Bs)
        Sib[k * nB + b, a] = keep[...]

    def stage3(i):
        k = order(i)
        for j in Bs:
            got(y2r.at[k, j], ry2, (k, j))
        for j in As:
            got(x2r.at[k, j], rx2, (k, j))
        keep[:, lo] = Sib[k * nB + b, a, :, lo] + sum(y2r[k, j].astype(f32) for j in Bs)
        keep[:, hi] = Sib[k * nB + b, a, :, hi] + sum(x2r[k, j].astype(f32) for j in As)

        @pl.when(i < nC - 1)
        def _():
            zb[k] = keep[...].astype(bf16)
            put(zb.at[k], zr.at[z], rz, k, z, at(z_=k))

    def reduce_step(i, carry):
        @pl.when(i < nC)
        def _():
            produce(i)

        @pl.when((i > 0) & (i < nC + 1))
        def _():
            stage1(i - 1)

        @pl.when((i > 1) & (i < nC + 2))
        def _():
            stage2(i - 2)

        @pl.when(i > 2)
        def _():
            stage3(i - 3)

        return carry

    lax.fori_loop(0, nC + 3, reduce_step, 0)
    for k in Zs:
        got(zr.at[k], rz, k)
    grad_out[...] = keep[...] + sum(zr[k].astype(f32) for k in Zs)

    for k in Zs:
        sent(zb.at[k], rz, k)

    def drain(k, carry):
        own = slot(k, b, a)

        @pl.when((k <= z) & (z < nC - 1))
        def _():
            sent(own, gz, (k, 1))

        @pl.when((k >= z) & (z > 0))
        def _():
            sent(own, gz, (k, 0))

        for j in As:
            sent(own, gx1, (k, j))
            sent(x1b.at[k, j], rx1, (k, j))
            sent(x2b.at[k, j], rx2, (k, j))
        for j in Bs:
            sent(own, gy1, (k, j))
            sent(y1b.at[k, j], ry1, (k, j))
            sent(y2b.at[k, j], ry2, (k, j))
            for m in As:
                sent(own.at[:, lo], gy2, (k, j, m))
                sent(own.at[:, hi], gx2, (k, j, m))
        for b_ in range(nB):
            for a_ in range(nA):
                sent(own, gs, (k, b_, a_))
            sent(Sib.at[k * nB + b_], rs, k * nB + b_)
        return carry

    lax.fori_loop(0, nC, drain, 0)


def local(hidden, weight, targets, token_weight):
    rows, cols = hidden.shape
    n_pipe, n_tensor = lax.axis_size("pipe"), lax.axis_size("tensor")
    nA, nB, nC = n_pipe // 2, 2, n_tensor // 2
    tokens, width = targets.shape[0], weight.shape[1]
    half = cols // 2
    vmem, dma = pltpu.VMEM, pltpu.SemaphoreType.DMA
    sems = lambda *shape: [dma(shape), dma(shape)]
    groups = 2 * nA * nB + nC
    token_loss, hidden_grad = pl.pallas_call(
        functools.partial(kernel, nA, nB, nC),
        out_shape=(
            jax.ShapeDtypeStruct((rows,), f32),
            jax.ShapeDtypeStruct((rows, cols), f32),
        ),
        in_specs=[
            pl.BlockSpec(memory_space=pl.ANY),
            pl.BlockSpec(memory_space=pl.ANY),
            pl.BlockSpec(memory_space=vmem),
            pl.BlockSpec(memory_space=vmem),
        ],
        out_specs=[pl.BlockSpec(memory_space=vmem)] * 2,
        scratch_shapes=[
            vmem((n_tensor, n_pipe, rows, cols), bf16),
            vmem((n_tensor, cols, width), bf16),
            vmem((tokens, width), f32),
            vmem((tokens, width), bf16),
            vmem((n_tensor, nA, 2, rows, cols), f32),
            vmem((n_tensor, nA, rows, cols), f32),
            vmem((nC, nA, nB, rows, half), bf16),
            vmem((nC, nA, nB, rows, half), bf16),
            vmem((nC, nB, nA, rows, half), bf16),
            vmem((nC, nB, nA, rows, half), bf16),
            vmem((nC, nA, rows, half), bf16),
            vmem((nC, nA, rows, half), bf16),
            vmem((nC, nB, rows, half), bf16),
            vmem((nC, nB, rows, half), bf16),
            vmem((nC, rows, cols), bf16),
            vmem((nC, rows, cols), bf16),
            vmem((rows, cols), f32),
            vmem((2, 4, tokens), f32),
            vmem((groups, 4, tokens), f32),
            dma,
            dma,
            sems(nC, 2),
            sems(nC, nA),
            sems(nC, nB),
            sems(nC, nB, nA),
            sems(nC, nB, nA),
            sems(nC, nB, nA),
            sems(n_tensor),
            sems(nC, nA),
            sems(nC, nB),
            sems(nC, nA),
            sems(nC, nB),
            sems(nC),
            sems(groups),
        ],
        compiler_params=pltpu.CompilerParams(
            collective_id=0, has_side_effects=True, vmem_limit_bytes=62 * 1024 * 1024
        ),
    )(
        hidden,
        weight.reshape(n_tensor, cols, width),
        targets,
        token_weight,
    )
    return token_loss, hidden_grad


def solution(mesh):
    in_specs = (P("pipe", "tensor"), P(None, ("pipe", "tensor")), P(), P())
    out_specs = (P("pipe"), P("pipe", "tensor"))
    return jax.shard_map(local, mesh=mesh, in_specs=in_specs, out_specs=out_specs, check_vma=False)
```

```python
import functools

import jax
import jax.numpy as jnp
from jax import lax
from jax.experimental import pallas as pl
from jax.experimental.pallas import tpu as pltpu
from jax.sharding import PartitionSpec as P

loss_scale = 32.0
f32, bf16 = jnp.float32, jnp.bfloat16
MESH = pl.DeviceIdType.MESH


def flat_rows(block):
    n, rows, width = block.shape
    if rows % 16:
        return block.astype(f32).reshape(n * rows, width).astype(bf16)
    return block.reshape(n * rows, width)


def to_column(row):
    return jnp.transpose(jnp.broadcast_to(row, (128, row.shape[1])))[:, :1]


def merge(parts):
    peak = functools.reduce(jnp.maximum, [part[0:1] for part in parts])
    total = sum(part[1:2] * jnp.exp(part[0:1] - peak) for part in parts)
    chosen = sum(part[2:3] for part in parts)
    return jnp.concatenate([peak, total, chosen, jnp.zeros_like(peak)], axis=0)


def kernel(
    nA, nB, nC, nH,
    hidden, weight, targets, token_weight,
    loss_out, grad_out,
    H, W, acc, dl, Pb, Sib, x1b, x1r, y1b, y1r, x2b, x2r, y2b, y2r, zb, zr, keep, stb, st, lossb,
    wsem, hsem, gz, gx1, gy1, gx2, gy2, gs, rs, rx1, ry1, rx2, ry2, rz, ssem,
):
    rows, cols = hidden.shape
    chunk = rows // nH
    half = cols // 2
    lo, hi = pl.ds(0, half), pl.ds(half, half)
    p, t = lax.axis_index("pipe"), lax.axis_index("tensor")
    a, c = p // 2, lax.rem(p, 2)
    b, z = lax.rem(t, nB), t // nB

    def at(a_=None, b_=None, z_=None, c_=None):
        a_, b_ = (a if a_ is None else a_), (b if b_ is None else b_)
        z_, c_ = (z if z_ is None else z_), (c if c_ is None else c_)
        return {"pipe": a_ * 2 + c_, "tensor": z_ * nB + b_}

    As = [lax.rem(a + o, nA) for o in range(1, nA)]
    Bs = [lax.rem(b + o, nB) for o in range(1, nB)]
    Zs = [lax.rem(z - o + nC, nC) for o in range(1, nC)]
    sib = at(c_=1 - c)
    Plane = [
        ((a_ * nB + b_) * 2 + c_, at(a_=a_, b_=b_, c_=c_))
        for a_ in [a] + As for b_ in [b] + Bs for c_ in (c, 1 - c)
    ][1:]
    peers = [dev for _, dev in Plane] + [at(z_=i) for i in Zs]

    def put(src, dst, sems, here, there, dev):
        pltpu.make_async_remote_copy(
            src_ref=src, dst_ref=dst, send_sem=sems[0].at[here], recv_sem=sems[1].at[there],
            device_id=dev, device_id_type=MESH,
        ).start()

    def got(dst, sems, there):
        pltpu.make_async_remote_copy(
            src_ref=dst, dst_ref=dst, send_sem=sems[0].at[there], recv_sem=sems[1].at[there],
            device_id=sib, device_id_type=MESH,
        ).wait_recv()

    def sent(src, sems, here):
        pltpu.make_async_remote_copy(
            src_ref=src, dst_ref=src, send_sem=sems[0].at[here], recv_sem=sems[1].at[here],
            device_id=sib, device_id_type=MESH,
        ).wait_send()

    wcopy = pltpu.make_async_copy(weight, W, wsem)
    hcopies = [
        pltpu.make_async_copy(hidden.at[pl.ds(h * chunk, chunk)], H.at[h, t, p], hsem.at[h])
        for h in range(nH)
    ]
    for copy in hcopies:
        copy.start()
    wcopy.start()
    barrier = pltpu.get_barrier_semaphore()
    for dev in peers:
        pl.semaphore_signal(barrier, inc=1, device_id=dev, device_id_type=MESH)
    for copy in hcopies:
        copy.wait()
    acc[...] = jnp.zeros_like(acc)
    target_col = to_column(targets[...].reshape(1, -1).astype(f32)).astype(jnp.int32)
    scale_col = loss_scale * to_column(token_weight[...].reshape(1, -1))
    pl.semaphore_wait(barrier, len(peers))

    def slot(h, k, b_, a_, c_=None):
        return H.at[h, k * nB + b_, a_ * 2 + (c if c_ is None else c_)]

    left, right = z, nC - 1 - z
    both = jnp.minimum(left, right)
    longer = jnp.where(left > right, -1, 1)

    def nearest(step):
        h, i = step // nC, lax.rem(step, nC)
        d = (i + 1) // 2
        turn = jnp.where(lax.rem(i, 2) == 1, -d, d)
        return h, z + jnp.where(i <= 2 * both, turn, longer * (i - both))

    def spread(step):
        h, k = nearest(step)
        own = slot(h, k, b, a)

        @pl.when(k != z)
        def _():
            got(own, gz, (h, k, 0))

        @pl.when((k <= z) & (z < nC - 1))
        def _():
            put(own, own, gz, (h, k, 1), (h, k, 0), at(z_=z + 1))

        @pl.when((k >= z) & (z > 0))
        def _():
            put(own, own, gz, (h, k, 0), (h, k, 0), at(z_=z - 1))

        for j in As:
            put(own, own, gx1, (h, k, j), (h, k, a), at(a_=j))
        for j in Bs:
            put(own, own, gy1, (h, k, j), (h, k, b), at(b_=j))
        put(own, own, gs, (h, k, b, a), (h, k, b, a), sib)

    def forward(step):
        h, k = nearest(step)
        for j in As:
            blk = slot(h, k, b, j)
            got(blk, gx1, (h, k, j))
            for m in Bs:
                put(blk.at[:, lo], blk.at[:, lo], gy2, (h, k, m, j), (h, k, b, j), at(b_=m))
        for j in Bs:
            blk = slot(h, k, j, a)
            got(blk, gy1, (h, k, j))
            for m in As:
                put(blk.at[:, hi], blk.at[:, hi], gx2, (h, k, j, m), (h, k, j, a), at(a_=m))
        for j in As:
            blk = slot(h, k, b, j)
            put(blk, blk, gs, (h, k, b, j), (h, k, b, j), sib)
        for j in Bs:
            blk = slot(h, k, j, a)
            put(blk, blk, gs, (h, k, j, a), (h, k, j, a), sib)

    def finish(step):
        h, k = nearest(step)
        for j in As:
            for m in Bs:
                blk = slot(h, k, m, j)
                got(blk.at[:, lo], gy2, (h, k, m, j))
                got(blk.at[:, hi], gx2, (h, k, m, j))
                put(blk, blk, gs, (h, k, m, j), (h, k, m, j), sib)

    def multiply(step):
        h, k = nearest(step)
        for b_ in range(nB):
            for a_ in range(nA):
                got(slot(h, k, b_, a_, 1 - c), gs, (h, k, b_, a_))
        for b_ in range(nB):
            tt = k * nB + b_
            acc[h] += jnp.dot(flat_rows(H[h, tt]), W[tt], preferred_element_type=f32)

    tokens, width = acc.shape[1:]
    padded = stb.shape[-1]
    device_block = p * lax.axis_size("tensor") + t
    plane = nA * nB * 2
    groups = (
        (Plane, 0, (a * nB + b) * 2 + c),
        ([(k, at(z_=k)) for k in Zs], plane, z),
    )

    def of_chunk(column, h):
        sections = nA * 2
        return column.reshape(sections, nH, chunk, 1)[:, h].reshape(sections * chunk, 1)

    def hits(h):
        columns = device_block * width + lax.broadcasted_iota(jnp.int32, (tokens, width), 1)
        return of_chunk(target_col, h) == columns

    def share(h, stage, mine):
        group, base, me = groups[stage]
        stb[h, stage] = mine
        for j, dev in group:
            put(stb.at[h, stage], st.at[h, base + me], ssem, (h, base + j), (h, base + me), dev)

    def merged(h, stage):
        group, base, me = groups[stage]
        for j, _ in group:
            got(st.at[h, base + j], ssem, (h, base + j))
        return merge([stb[h, stage]] + [st[h, base + j] for j, _ in group])

    def stats_local(h):
        logits = acc[h]
        peak = jnp.max(logits, axis=1, keepdims=True)
        total = jnp.sum(jnp.exp(logits - peak), axis=1, keepdims=True)
        chosen = jnp.sum(jnp.where(hits(h), logits, 0.0), axis=1, keepdims=True)
        lane = lax.broadcasted_iota(jnp.int32, (tokens, 128), 1)
        packed = jnp.where(
            lane == 0, peak, jnp.where(lane == 1, total, jnp.where(lane == 2, chosen, 0.0))
        )
        if padded > tokens:
            packed = jnp.concatenate([packed, jnp.zeros((padded - tokens, 128), f32)], axis=0)
        share(h, 0, jnp.transpose(packed)[0:4])

    def stats_plane(h):
        share(h, 1, merged(h, 0))

    def stats_line(h):
        cur = merged(h, 1)
        log_total = cur[0:1] + jnp.log(cur[1:2])
        loss = jnp.broadcast_to(log_total - cur[2:3], (8, padded))
        lossb[h] = pltpu.roll(loss, lax.rem((h - p) * chunk + nA * 2 * padded, padded), axis=1)
        softmax = jnp.exp(acc[h] - to_column(log_total)[:tokens])
        dl[h] = (of_chunk(scale_col, h) * (softmax - hits(h).astype(f32))).astype(bf16)

    def order(step):
        return step // nC, lax.rem(z + 1 + lax.rem(step, nC), nC)

    def produce(step):
        h, k = order(step)
        for b_ in range(nB):
            tt = k * nB + b_
            for part in (lo, hi):
                term = lax.dot_general(
                    dl[h], W[tt, part, :], (((1,), (1,)), ((), ())), preferred_element_type=f32
                )
                Pb[h, tt, :, :, :, part] = term.reshape(nA, 2, chunk, half)
            put(Pb.at[h, tt, :, 1 - c], Sib.at[h, tt], rs, (h, tt), (h, tt), sib)

    def stage1(step):
        h, k = order(step)
        for b_ in range(nB):
            tt = k * nB + b_
            got(Sib.at[h, tt], rs, (h, tt))
            for a_ in range(nA):
                Sib[h, tt, a_] = Sib[h, tt, a_] + Pb[h, tt, a_, c]
        for j in As:
            for b_ in range(nB):
                x1b[h, k, j, b_] = Sib[h, k * nB + b_, j, :, lo].astype(bf16)
            put(x1b.at[h, k, j], x1r.at[h, k, a], rx1, (h, k, j), (h, k, a), at(a_=j))
        for j in Bs:
            for a_ in range(nA):
                y1b[h, k, j, a_] = Sib[h, k * nB + j, a_, :, hi].astype(bf16)
            put(y1b.at[h, k, j], y1r.at[h, k, b], ry1, (h, k, j), (h, k, b), at(b_=j))

    def stage2(step):
        h, k = order(step)
        tb = k * nB + b
        for j in As:
            got(x1r.at[h, k, j], rx1, (h, k, j))
        for j in Bs:
            term = sum(x1r[h, k, m, j].astype(f32) for m in As)
            y2b[h, k, j] = (Sib[h, k * nB + j, a, :, lo] + term).astype(bf16)
            put(y2b.at[h, k, j], y2r.at[h, k, b], ry2, (h, k, j), (h, k, b), at(b_=j))
        for j in Bs:
            got(y1r.at[h, k, j], ry1, (h, k, j))
        for j in As:
            term = sum(y1r[h, k, m, j].astype(f32) for m in Bs)
            x2b[h, k, j] = (Sib[h, tb, j, :, hi] + term).astype(bf16)
            put(x2b.at[h, k, j], x2r.at[h, k, a], rx2, (h, k, j), (h, k, a), at(a_=j))
        Sib[h, tb, a, :, lo] = Sib[h, tb, a, :, lo] + sum(x1r[h, k, m, b].astype(f32) for m in As)
        Sib[h, tb, a, :, hi] = Sib[h, tb, a, :, hi] + sum(y1r[h, k, m, a].astype(f32) for m in Bs)

    def stage3(step):
        h, k = order(step)
        tb = k * nB + b
        for j in Bs:
            got(y2r.at[h, k, j], ry2, (h, k, j))
        for j in As:
            got(x2r.at[h, k, j], rx2, (h, k, j))
        keep[h, :, lo] = Sib[h, tb, a, :, lo] + sum(y2r[h, k, j].astype(f32) for j in Bs)
        keep[h, :, hi] = Sib[h, tb, a, :, hi] + sum(x2r[h, k, j].astype(f32) for j in As)

        @pl.when(lax.rem(step, nC) < nC - 1)
        def _():
            zb[h, k] = keep[h].astype(bf16)
            put(zb.at[h, k], zr.at[h, z], rz, (h, k), (h, z), at(z_=k))

    steps = nH * nC
    offset = nC + 4

    def during(i, first, count, action, lag):
        @pl.when((i >= first + lag) & (i < first + lag + count))
        def _():
            action(i - first - lag)

    def once(i, when, action, h):
        @pl.when(i == when)
        def _():
            action(h)

    spread(0)

    def step(i, carry):
        during(i, 0, steps - 1, lambda n: spread(n + 1), 0)
        during(i, 0, steps, forward, 0)

        @pl.when(i == 2)
        def _():
            wcopy.wait()

        during(i, offset, steps, produce, 0)
        during(i, offset, steps, stage1, 1)
        during(i, offset, steps, stage2, 2)
        during(i, offset, steps, stage3, 3)
        during(i, 0, steps, finish, 2)
        during(i, 0, steps, multiply, 2)
        for h in range(nH):
            once(i, (h + 1) * nC + 1, stats_local, h)
            once(i, (h + 1) * nC + 2, stats_plane, h)
            once(i, (h + 1) * nC + 3, stats_line, h)
        return carry

    lax.fori_loop(0, offset + steps + 3, step, 0)
    lane = lax.broadcasted_iota(jnp.int32, (8, padded), 1)
    loss = lossb[0]
    for h in range(1, nH):
        loss = jnp.where(lane >= h * chunk, lossb[h], loss)
    loss_out[...] = loss[0, :rows]
    for h in range(nH):
        for k in Zs:
            got(zr.at[h, k], rz, (h, k))
        grad_out[pl.ds(h * chunk, chunk), :] = keep[h] + sum(zr[h, k].astype(f32) for k in Zs)

    for h in range(nH):
        for k in Zs:
            sent(zb.at[h, k], rz, (h, k))
        for stage, (group, base, _) in enumerate(groups):
            for j, _ in group:
                sent(stb.at[h, stage], ssem, (h, base + j))

    def drain(n, carry):
        h, k = n // nC, lax.rem(n, nC)
        own = slot(h, k, b, a)

        @pl.when((k <= z) & (z < nC - 1))
        def _():
            sent(own, gz, (h, k, 1))

        @pl.when((k >= z) & (z > 0))
        def _():
            sent(own, gz, (h, k, 0))

        for j in As:
            sent(own, gx1, (h, k, j))
            sent(x1b.at[h, k, j], rx1, (h, k, j))
            sent(x2b.at[h, k, j], rx2, (h, k, j))
        for j in Bs:
            sent(own, gy1, (h, k, j))
            sent(y1b.at[h, k, j], ry1, (h, k, j))
            sent(y2b.at[h, k, j], ry2, (h, k, j))
            for m in As:
                sent(own.at[:, lo], gy2, (h, k, j, m))
                sent(own.at[:, hi], gx2, (h, k, j, m))
        for b_ in range(nB):
            for a_ in range(nA):
                sent(own, gs, (h, k, b_, a_))
            sent(Sib.at[h, k * nB + b_], rs, (h, k * nB + b_))
        return carry

    lax.fori_loop(0, steps, drain, 0)


def local(hidden, weight, targets, token_weight):
    rows, cols = hidden.shape
    n_pipe, n_tensor = lax.axis_size("pipe"), lax.axis_size("tensor")
    nA, nB, nC = n_pipe // 2, 2, n_tensor // 2
    tokens, width = targets.shape[0], weight.shape[1]
    half = cols // 2
    vmem, dma = pltpu.VMEM, pltpu.SemaphoreType.DMA
    sems = lambda *shape: [dma(shape), dma(shape)]
    groups = 2 * nA * nB + nC
    nH = 2 if rows % 32 == 0 else 1
    chunk = rows // nH
    part = n_pipe * chunk
    padded = -(-part // 128) * 128
    token_loss, hidden_grad = pl.pallas_call(
        functools.partial(kernel, nA, nB, nC, nH),
        out_shape=(
            jax.ShapeDtypeStruct((rows,), f32),
            jax.ShapeDtypeStruct((rows, cols), f32),
        ),
        in_specs=[
            pl.BlockSpec(memory_space=pl.ANY),
            pl.BlockSpec(memory_space=pl.ANY),
            pl.BlockSpec(memory_space=vmem),
            pl.BlockSpec(memory_space=vmem),
        ],
        out_specs=[pl.BlockSpec(memory_space=vmem)] * 2,
        scratch_shapes=[
            vmem((nH, n_tensor, n_pipe, chunk, cols), bf16),
            vmem((n_tensor, cols, width), bf16),
            vmem((nH, part, width), f32),
            vmem((nH, part, width), bf16),
            vmem((nH, n_tensor, nA, 2, chunk, cols), f32),
            vmem((nH, n_tensor, nA, chunk, cols), f32),
            vmem((nH, nC, nA, nB, chunk, half), bf16),
            vmem((nH, nC, nA, nB, chunk, half), bf16),
            vmem((nH, nC, nB, nA, chunk, half), bf16),
            vmem((nH, nC, nB, nA, chunk, half), bf16),
            vmem((nH, nC, nA, chunk, half), bf16),
            vmem((nH, nC, nA, chunk, half), bf16),
            vmem((nH, nC, nB, chunk, half), bf16),
            vmem((nH, nC, nB, chunk, half), bf16),
            vmem((nH, nC, chunk, cols), bf16),
            vmem((nH, nC, chunk, cols), bf16),
            vmem((nH, chunk, cols), f32),
            vmem((nH, 2, 4, padded), f32),
            vmem((nH, groups, 4, padded), f32),
            vmem((nH, 8, padded), f32),
            dma,
            dma((nH,)),
            sems(nH, nC, 2),
            sems(nH, nC, nA),
            sems(nH, nC, nB),
            sems(nH, nC, nB, nA),
            sems(nH, nC, nB, nA),
            sems(nH, nC, nB, nA),
            sems(nH, n_tensor),
            sems(nH, nC, nA),
            sems(nH, nC, nB),
            sems(nH, nC, nA),
            sems(nH, nC, nB),
            sems(nH, nC),
            sems(nH, groups),
        ],
        compiler_params=pltpu.CompilerParams(
            collective_id=0, has_side_effects=True, vmem_limit_bytes=62 * 1024 * 1024
        ),
    )(
        hidden,
        weight.reshape(n_tensor, cols, width),
        targets,
        token_weight,
    )
    return token_loss, hidden_grad


def solution(mesh):
    in_specs = (P("pipe", "tensor"), P(None, ("pipe", "tensor")), P(), P())
    out_specs = (P("pipe"), P("pipe", "tensor"))
    return jax.shard_map(local, mesh=mesh, in_specs=in_specs, out_specs=out_specs, check_vma=False)
```

```python
import functools

import jax
import jax.numpy as jnp
from jax import lax
from jax.experimental import pallas as pl
from jax.experimental.pallas import tpu as pltpu
from jax.sharding import PartitionSpec as P

loss_scale = 32.0
f32, bf16 = jnp.float32, jnp.bfloat16
MESH = pl.DeviceIdType.MESH


def flat_rows(block):
    n, rows, width = block.shape
    if rows % 16:
        return block.astype(f32).reshape(n * rows, width).astype(bf16)
    return block.reshape(n * rows, width)


def to_column(row):
    return jnp.transpose(jnp.broadcast_to(row, (128, row.shape[1])))[:, :1]


def merge(parts):
    peak = functools.reduce(jnp.maximum, [part[0:1] for part in parts])
    total = sum(part[1:2] * jnp.exp(part[0:1] - peak) for part in parts)
    chosen = sum(part[2:3] for part in parts)
    return jnp.concatenate([peak, total, chosen, jnp.zeros_like(peak)], axis=0)


def kernel(
    nA, nB, nC, nH,
    hidden, weight, targets, token_weight,
    loss_out, grad_out,
    H, W, acc, dl, Pb, Sib, x1b, x1r, y1b, y1r, x2b, x2r, y2b, y2r, zb, zr, keep, stb, st, lossb,
    wsem, hsem, gz, gx1, gy1, gx2, gy2, gs, rs, rx1, ry1, rx2, ry2, rz, ssem,
):
    rows, cols = hidden.shape
    chunk = rows // nH
    half = cols // 2
    lo, hi = pl.ds(0, half), pl.ds(half, half)
    p, t = lax.axis_index("pipe"), lax.axis_index("tensor")
    a, c = p // 2, lax.rem(p, 2)
    b, z = lax.rem(t, nB), t // nB

    def at(a_=None, b_=None, z_=None, c_=None):
        a_, b_ = (a if a_ is None else a_), (b if b_ is None else b_)
        z_, c_ = (z if z_ is None else z_), (c if c_ is None else c_)
        return {"pipe": a_ * 2 + c_, "tensor": z_ * nB + b_}

    As = [lax.rem(a + o, nA) for o in range(1, nA)]
    Bs = [lax.rem(b + o, nB) for o in range(1, nB)]
    Zs = [lax.rem(z - o + nC, nC) for o in range(1, nC)]
    sib = at(c_=1 - c)
    Plane = [
        ((a_ * nB + b_) * 2 + c_, at(a_=a_, b_=b_, c_=c_))
        for a_ in [a] + As for b_ in [b] + Bs for c_ in (c, 1 - c)
    ][1:]
    peers = [dev for _, dev in Plane] + [at(z_=i) for i in Zs]

    def put(src, dst, sems, here, there, dev):
        pltpu.make_async_remote_copy(
            src_ref=src, dst_ref=dst, send_sem=sems[0].at[here], recv_sem=sems[1].at[there],
            device_id=dev, device_id_type=MESH,
        ).start()

    def got(dst, sems, there):
        pltpu.make_async_remote_copy(
            src_ref=dst, dst_ref=dst, send_sem=sems[0].at[there], recv_sem=sems[1].at[there],
            device_id=sib, device_id_type=MESH,
        ).wait_recv()

    def sent(src, sems, here):
        pltpu.make_async_remote_copy(
            src_ref=src, dst_ref=src, send_sem=sems[0].at[here], recv_sem=sems[1].at[here],
            device_id=sib, device_id_type=MESH,
        ).wait_send()

    wcopy = pltpu.make_async_copy(weight, W, wsem)
    hcopies = [
        pltpu.make_async_copy(hidden.at[pl.ds(h * chunk, chunk)], H.at[h, t, p], hsem.at[h])
        for h in range(nH)
    ]
    for copy in hcopies:
        copy.start()
    wcopy.start()
    barrier = pltpu.get_barrier_semaphore()
    for dev in peers:
        pl.semaphore_signal(barrier, inc=1, device_id=dev, device_id_type=MESH)
    for copy in hcopies:
        copy.wait()
    acc[...] = jnp.zeros_like(acc)
    target_col = to_column(targets[...].reshape(1, -1).astype(f32)).astype(jnp.int32)
    scale_col = loss_scale * to_column(token_weight[...].reshape(1, -1))
    pl.semaphore_wait(barrier, len(peers))

    def slot(h, k, b_, a_, c_=None):
        return H.at[h, k * nB + b_, a_ * 2 + (c if c_ is None else c_)]

    left, right = z, nC - 1 - z
    both = jnp.minimum(left, right)
    longer = jnp.where(left > right, -1, 1)

    def nearest(step):
        h, i = step // nC, lax.rem(step, nC)
        d = (i + 1) // 2
        turn = jnp.where(lax.rem(i, 2) == 1, -d, d)
        return h, z + jnp.where(i <= 2 * both, turn, longer * (i - both))

    def spread(step):
        h, k = nearest(step)
        own = slot(h, k, b, a)

        @pl.when(k != z)
        def _():
            got(own, gz, (h, k, 0))

        @pl.when((k <= z) & (z < nC - 1))
        def _():
            put(own, own, gz, (h, k, 1), (h, k, 0), at(z_=z + 1))

        @pl.when((k >= z) & (z > 0))
        def _():
            put(own, own, gz, (h, k, 0), (h, k, 0), at(z_=z - 1))

        for j in As:
            put(own, own, gx1, (h, k, j), (h, k, a), at(a_=j))
        for j in Bs:
            put(own, own, gy1, (h, k, j), (h, k, b), at(b_=j))
        put(own, own, gs, (h, k, b, a), (h, k, b, a), sib)

    def forward(step):
        h, k = nearest(step)
        for j in As:
            blk = slot(h, k, b, j)
            got(blk, gx1, (h, k, j))
            for m in Bs:
                put(blk.at[:, lo], blk.at[:, lo], gy2, (h, k, m, j), (h, k, b, j), at(b_=m))
        for j in Bs:
            blk = slot(h, k, j, a)
            got(blk, gy1, (h, k, j))
            for m in As:
                put(blk.at[:, hi], blk.at[:, hi], gx2, (h, k, j, m), (h, k, j, a), at(a_=m))
        for j in As:
            blk = slot(h, k, b, j)
            put(blk, blk, gs, (h, k, b, j), (h, k, b, j), sib)
        for j in Bs:
            blk = slot(h, k, j, a)
            put(blk, blk, gs, (h, k, j, a), (h, k, j, a), sib)

    def finish(step):
        h, k = nearest(step)
        for j in As:
            for m in Bs:
                blk = slot(h, k, m, j)
                got(blk.at[:, lo], gy2, (h, k, m, j))
                got(blk.at[:, hi], gx2, (h, k, m, j))
                put(blk, blk, gs, (h, k, m, j), (h, k, m, j), sib)

    def multiply(step):
        h, k = nearest(step)
        for b_ in range(nB):
            for a_ in range(nA):
                got(slot(h, k, b_, a_, 1 - c), gs, (h, k, b_, a_))
        for b_ in range(nB):
            tt = k * nB + b_
            acc[h] += jnp.dot(flat_rows(H[h, tt]), W[tt], preferred_element_type=f32)

    tokens, width = acc.shape[1:]
    padded = stb.shape[-1]
    device_block = p * lax.axis_size("tensor") + t
    plane = nA * nB * 2
    groups = (
        (Plane, 0, (a * nB + b) * 2 + c),
        ([(k, at(z_=k)) for k in Zs], plane, z),
    )

    def of_chunk(column, h):
        sections = nA * 2
        return column.reshape(sections, nH, chunk, 1)[:, h].reshape(sections * chunk, 1)

    def hits(h):
        columns = device_block * width + lax.broadcasted_iota(jnp.int32, (tokens, width), 1)
        return of_chunk(target_col, h) == columns

    def share(h, stage, mine):
        group, base, me = groups[stage]
        stb[h, stage] = mine
        for j, dev in group:
            put(stb.at[h, stage], st.at[h, base + me], ssem, (h, base + j), (h, base + me), dev)

    def merged(h, stage):
        group, base, me = groups[stage]
        for j, _ in group:
            got(st.at[h, base + j], ssem, (h, base + j))
        return merge([stb[h, stage]] + [st[h, base + j] for j, _ in group])

    def stats_local(h):
        logits = acc[h]
        peak = jnp.max(logits, axis=1, keepdims=True)
        total = jnp.sum(jnp.exp(logits - peak), axis=1, keepdims=True)
        chosen = jnp.sum(jnp.where(hits(h), logits, 0.0), axis=1, keepdims=True)
        lane = lax.broadcasted_iota(jnp.int32, (tokens, 128), 1)
        packed = jnp.where(
            lane == 0, peak, jnp.where(lane == 1, total, jnp.where(lane == 2, chosen, 0.0))
        )
        if padded > tokens:
            packed = jnp.concatenate([packed, jnp.zeros((padded - tokens, 128), f32)], axis=0)
        share(h, 0, jnp.transpose(packed)[0:4])

    def stats_plane(h):
        share(h, 1, merged(h, 0))

    def stats_line(h):
        cur = merged(h, 1)
        log_total = cur[0:1] + jnp.log(cur[1:2])
        loss = jnp.broadcast_to(log_total - cur[2:3], (8, padded))
        lossb[h] = pltpu.roll(loss, lax.rem((h - p) * chunk + nA * 2 * padded, padded), axis=1)
        softmax = jnp.exp(acc[h] - to_column(log_total)[:tokens])
        dl[h] = (of_chunk(scale_col, h) * (softmax - hits(h).astype(f32))).astype(bf16)

    def order(step):
        return step // nC, lax.rem(z + 1 + lax.rem(step, nC), nC)

    def produce(step):
        h, k = order(step)
        for b_ in range(nB):
            tt = k * nB + b_
            for part in (lo, hi):
                term = lax.dot_general(
                    dl[h], W[tt, part, :], (((1,), (1,)), ((), ())), preferred_element_type=f32
                )
                Pb[h, tt, :, :, :, part] = term.reshape(nA, 2, chunk, half)
            put(Pb.at[h, tt, :, 1 - c], Sib.at[h, tt], rs, (h, tt), (h, tt), sib)

    def stage1(step):
        h, k = order(step)
        for b_ in range(nB):
            tt = k * nB + b_
            got(Sib.at[h, tt], rs, (h, tt))
            for a_ in range(nA):
                Sib[h, tt, a_] = Sib[h, tt, a_] + Pb[h, tt, a_, c]
        for j in As:
            for b_ in range(nB):
                x1b[h, k, j, b_] = Sib[h, k * nB + b_, j, :, lo].astype(bf16)
            put(x1b.at[h, k, j], x1r.at[h, k, a], rx1, (h, k, j), (h, k, a), at(a_=j))
        for j in Bs:
            for a_ in range(nA):
                y1b[h, k, j, a_] = Sib[h, k * nB + j, a_, :, hi].astype(bf16)
            put(y1b.at[h, k, j], y1r.at[h, k, b], ry1, (h, k, j), (h, k, b), at(b_=j))

    def stage2(step):
        h, k = order(step)
        tb = k * nB + b
        for j in As:
            got(x1r.at[h, k, j], rx1, (h, k, j))
        for j in Bs:
            term = sum(x1r[h, k, m, j].astype(f32) for m in As)
            y2b[h, k, j] = (Sib[h, k * nB + j, a, :, lo] + term).astype(bf16)
            put(y2b.at[h, k, j], y2r.at[h, k, b], ry2, (h, k, j), (h, k, b), at(b_=j))
        for j in Bs:
            got(y1r.at[h, k, j], ry1, (h, k, j))
        for j in As:
            term = sum(y1r[h, k, m, j].astype(f32) for m in Bs)
            x2b[h, k, j] = (Sib[h, tb, j, :, hi] + term).astype(bf16)
            put(x2b.at[h, k, j], x2r.at[h, k, a], rx2, (h, k, j), (h, k, a), at(a_=j))
        Sib[h, tb, a, :, lo] = Sib[h, tb, a, :, lo] + sum(x1r[h, k, m, b].astype(f32) for m in As)
        Sib[h, tb, a, :, hi] = Sib[h, tb, a, :, hi] + sum(y1r[h, k, m, a].astype(f32) for m in Bs)

    def stage3(step):
        h, k = order(step)
        tb = k * nB + b
        for j in Bs:
            got(y2r.at[h, k, j], ry2, (h, k, j))
        for j in As:
            got(x2r.at[h, k, j], rx2, (h, k, j))
        keep[h, :, lo] = Sib[h, tb, a, :, lo] + sum(y2r[h, k, j].astype(f32) for j in Bs)
        keep[h, :, hi] = Sib[h, tb, a, :, hi] + sum(x2r[h, k, j].astype(f32) for j in As)

        @pl.when(lax.rem(step, nC) < nC - 1)
        def _():
            zb[h, k] = keep[h].astype(bf16)
            put(zb.at[h, k], zr.at[h, z], rz, (h, k), (h, z), at(z_=k))

    steps = nH * nC
    offset = nC + 4

    def during(i, first, count, action, lag):
        @pl.when((i >= first + lag) & (i < first + lag + count))
        def _():
            action(i - first - lag)

    def once(i, when, action, h):
        @pl.when(i == when)
        def _():
            action(h)

    spread(0)

    def step(i, carry):
        during(i, 0, steps - 1, lambda n: spread(n + 1), 0)
        during(i, 0, steps, forward, 0)

        @pl.when(i == 2)
        def _():
            wcopy.wait()

        during(i, offset, steps, produce, 0)
        during(i, offset, steps, stage1, 1)
        during(i, offset, steps, stage2, 2)
        during(i, offset, steps, stage3, 3)
        during(i, 0, steps, multiply, 2)
        during(i, 0, steps, finish, 1)
        for h in range(nH):
            once(i, (h + 1) * nC + 1, stats_local, h)
            once(i, (h + 1) * nC + 2, stats_plane, h)
            once(i, (h + 1) * nC + 3, stats_line, h)
        return carry

    lax.fori_loop(0, offset + steps + 3, step, 0)
    lane = lax.broadcasted_iota(jnp.int32, (8, padded), 1)
    loss = lossb[0]
    for h in range(1, nH):
        loss = jnp.where(lane >= h * chunk, lossb[h], loss)
    loss_out[...] = loss[0, :rows]
    for h in range(nH):
        for k in Zs:
            got(zr.at[h, k], rz, (h, k))
        grad_out[pl.ds(h * chunk, chunk), :] = keep[h] + sum(zr[h, k].astype(f32) for k in Zs)

    for h in range(nH):
        for k in Zs:
            sent(zb.at[h, k], rz, (h, k))
        for stage, (group, base, _) in enumerate(groups):
            for j, _ in group:
                sent(stb.at[h, stage], ssem, (h, base + j))

    def drain(n, carry):
        h, k = n // nC, lax.rem(n, nC)
        own = slot(h, k, b, a)

        @pl.when((k <= z) & (z < nC - 1))
        def _():
            sent(own, gz, (h, k, 1))

        @pl.when((k >= z) & (z > 0))
        def _():
            sent(own, gz, (h, k, 0))

        for j in As:
            sent(own, gx1, (h, k, j))
            sent(x1b.at[h, k, j], rx1, (h, k, j))
            sent(x2b.at[h, k, j], rx2, (h, k, j))
        for j in Bs:
            sent(own, gy1, (h, k, j))
            sent(y1b.at[h, k, j], ry1, (h, k, j))
            sent(y2b.at[h, k, j], ry2, (h, k, j))
            for m in As:
                sent(own.at[:, lo], gy2, (h, k, j, m))
                sent(own.at[:, hi], gx2, (h, k, j, m))
        for b_ in range(nB):
            for a_ in range(nA):
                sent(own, gs, (h, k, b_, a_))
            sent(Sib.at[h, k * nB + b_], rs, (h, k * nB + b_))
        return carry

    lax.fori_loop(0, steps, drain, 0)


def local(hidden, weight, targets, token_weight):
    rows, cols = hidden.shape
    n_pipe, n_tensor = lax.axis_size("pipe"), lax.axis_size("tensor")
    nA, nB, nC = n_pipe // 2, 2, n_tensor // 2
    tokens, width = targets.shape[0], weight.shape[1]
    half = cols // 2
    vmem, dma = pltpu.VMEM, pltpu.SemaphoreType.DMA
    sems = lambda *shape: [dma(shape), dma(shape)]
    groups = 2 * nA * nB + nC
    nH = 2 if rows % 32 == 0 else 1
    chunk = rows // nH
    part = n_pipe * chunk
    padded = -(-part // 128) * 128
    token_loss, hidden_grad = pl.pallas_call(
        functools.partial(kernel, nA, nB, nC, nH),
        out_shape=(
            jax.ShapeDtypeStruct((rows,), f32),
            jax.ShapeDtypeStruct((rows, cols), f32),
        ),
        in_specs=[
            pl.BlockSpec(memory_space=pl.ANY),
            pl.BlockSpec(memory_space=pl.ANY),
            pl.BlockSpec(memory_space=vmem),
            pl.BlockSpec(memory_space=vmem),
        ],
        out_specs=[pl.BlockSpec(memory_space=vmem)] * 2,
        scratch_shapes=[
            vmem((nH, n_tensor, n_pipe, chunk, cols), bf16),
            vmem((n_tensor, cols, width), bf16),
            vmem((nH, part, width), f32),
            vmem((nH, part, width), bf16),
            vmem((nH, n_tensor, nA, 2, chunk, cols), f32),
            vmem((nH, n_tensor, nA, chunk, cols), f32),
            vmem((nH, nC, nA, nB, chunk, half), bf16),
            vmem((nH, nC, nA, nB, chunk, half), bf16),
            vmem((nH, nC, nB, nA, chunk, half), bf16),
            vmem((nH, nC, nB, nA, chunk, half), bf16),
            vmem((nH, nC, nA, chunk, half), bf16),
            vmem((nH, nC, nA, chunk, half), bf16),
            vmem((nH, nC, nB, chunk, half), bf16),
            vmem((nH, nC, nB, chunk, half), bf16),
            vmem((nH, nC, chunk, cols), bf16),
            vmem((nH, nC, chunk, cols), bf16),
            vmem((nH, chunk, cols), f32),
            vmem((nH, 2, 4, padded), f32),
            vmem((nH, groups, 4, padded), f32),
            vmem((nH, 8, padded), f32),
            dma,
            dma((nH,)),
            sems(nH, nC, 2),
            sems(nH, nC, nA),
            sems(nH, nC, nB),
            sems(nH, nC, nB, nA),
            sems(nH, nC, nB, nA),
            sems(nH, nC, nB, nA),
            sems(nH, n_tensor),
            sems(nH, nC, nA),
            sems(nH, nC, nB),
            sems(nH, nC, nA),
            sems(nH, nC, nB),
            sems(nH, nC),
            sems(nH, groups),
        ],
        compiler_params=pltpu.CompilerParams(
            collective_id=0, has_side_effects=True, vmem_limit_bytes=62 * 1024 * 1024
        ),
    )(
        hidden,
        weight.reshape(n_tensor, cols, width),
        targets,
        token_weight,
    )
    return token_loss, hidden_grad


def solution(mesh):
    in_specs = (P("pipe", "tensor"), P(None, ("pipe", "tensor")), P(), P())
    out_specs = (P("pipe"), P("pipe", "tensor"))
    return jax.shard_map(local, mesh=mesh, in_specs=in_specs, out_specs=out_specs, check_vma=False)
```
